32 devices in a mesh: orb: 8 (over y, x, core), pan: 4 (over z).
Axes of the slice: x: 2, y: 2, z: 4, core: 2. Of those that a mesh axis runs over, the one named last changes fastest.
Arguments:
- orbitals: float32 [128, 110592], P(('orb', 'pan')), may hold values from -6 to 6
- potential: float32 [110592], replicated, may hold values from -1 to 2
- magic_taps: float32 [16], replicated, may hold values from -4 to 4
- kinetic_taps: float32 [29], replicated, may hold values from -3 to 3
Outputs:
- gradient: float32 [128, 110592], P(('orb', 'pan'))
The draws below stay inside these ranges and needn't reach their ends.
All inputs are finite; a program needn't handle non-finite values.
Results may differ from the reference program's by a relative error of at most 0.00013.
Values sent between devices are 32-bit elements; how exact they have to be, the bound alone decides.
A program may use at most 128 MiB of HBM per device.

```python
import jax
import jax.numpy as jnp
from jax import lax

G = 48
MAGIC_TAPS = 16
KIN_TAPS = 29
NC = 110592
NORB = 128
N_PAN = 4


def level_of(stream_key, shape, shards, least, high):
    factor_of, own = 1.0, jax.random.fold_in(stream_key, 6)
    for position, shards_of in shards:
        draws = jnp.exp(jax.random.uniform(jax.random.fold_in(own, position), (shards_of,), jnp.float32, least / len(shards), high / len(shards)))
        factor_of = factor_of * jnp.repeat(draws, shape[position] // shards_of).reshape([-1 if axis == position else 1 for axis in range(len(shape))])
    return factor_of


def scatter_about(key, dims, spread, limit, shards=(), kind=jnp.bfloat16):
    drawn = jax.random.normal(key, dims, jnp.float32) * spread
    if len(shards) > 0:
        drawn = level_of(key, dims, shards, -0.22, 0.18) * drawn
    return jnp.clip(drawn, min=-limit, max=limit).astype(kind)


def setup_inputs(seed: int = 0) -> dict:
    streams_of = jax.random.split(jax.random.key(seed), 5)
    orbitals = scatter_about(streams_of[0], (NORB, NC), 1.0, 6.0, ((0, 32),), jnp.float32)
    potential = jnp.clip(jax.random.uniform(streams_of[1], (NC,), jnp.float32, -1.0, 2.0), -1.0, 2.0)
    magic_taps = scatter_about(streams_of[2], (MAGIC_TAPS,), 0.25, 4.0, (), jnp.float32)
    kinetic_taps = scatter_about(streams_of[3], (KIN_TAPS,), 0.2, 3.0, (), jnp.float32)
    return dict(orbitals=orbitals, potential=potential, magic_taps=magic_taps, kinetic_taps=kinetic_taps)


def filter_matrix(tap_values, extent):
    tap_count = tap_values.shape[0]
    centre = (tap_count - 1) // 2
    tap_ids = lax.broadcasted_iota(jnp.int32, (tap_count, extent, extent), 0)
    row_ids = lax.broadcasted_iota(jnp.int32, (tap_count, extent, extent), 1)
    col_ids = lax.broadcasted_iota(jnp.int32, (tap_count, extent, extent), 2)
    offset = (col_ids - row_ids - (tap_ids - centre)) % extent
    return jnp.sum(jnp.where(offset == 0, tap_values[:, None, None], jnp.float32(0.0)), axis=0)


def along(matrix, volume, which_axis):
    patterns = {1: "ab,nbcd->nacd", 2: "ab,ncbd->ncad", 3: "ab,ncdb->ncda"}
    return jnp.einsum(patterns[which_axis], matrix, volume, precision=lax.Precision.HIGHEST)


def hamiltonian(block, potential, magic_matrix, kinetic_matrix):
    count_here = block.shape[0]
    volume = block.reshape(count_here, G, G, G)
    smooth = volume
    for which_axis in (1, 2, 3):
        smooth = along(magic_matrix, smooth, which_axis)
    smooth = smooth * potential.reshape(1, G, G, G)
    for which_axis in (1, 2, 3):
        smooth = along(magic_matrix.T, smooth, which_axis)
    kinetic_part = along(kinetic_matrix, volume, 1) + along(kinetic_matrix, volume, 2) + along(kinetic_matrix, volume, 3)
    return (smooth + kinetic_part).reshape(count_here, G * G * G)


def reference(orbitals, potential, magic_taps, kinetic_taps):
    magic_matrix = filter_matrix(magic_taps, G)
    kinetic_matrix = filter_matrix(kinetic_taps, G)
    blocks = orbitals.reshape(N_PAN, -1, NC)
    hpsi = lax.map(lambda block: hamiltonian(block, potential, magic_matrix, kinetic_matrix), blocks).reshape(NORB, NC)
    margin = jnp.einsum("jc,ic->ji", orbitals, hpsi, precision=lax.Precision.HIGHEST) * (1.0 / NC)
    rotated = jnp.einsum("ji,jc->ic", margin, orbitals, precision=lax.Precision.HIGHEST)
    return hpsi - rotated
```

```python
import functools

import jax
import jax.numpy as jnp
import numpy as np
from jax import lax
from jax.experimental import pallas as pl
from jax.experimental.pallas import tpu as pltpu
from jax.sharding import PartitionSpec as P

G = 48
NC = 110592


def filter_matrix(tap_values, extent):
    tap_count = tap_values.shape[0]
    centre = (tap_count - 1) // 2
    tap_ids = lax.broadcasted_iota(jnp.int32, (tap_count, extent, extent), 0)
    row_ids = lax.broadcasted_iota(jnp.int32, (tap_count, extent, extent), 1)
    col_ids = lax.broadcasted_iota(jnp.int32, (tap_count, extent, extent), 2)
    offset = (col_ids - row_ids - (tap_ids - centre)) % extent
    return jnp.sum(jnp.where(offset == 0, tap_values[:, None, None], jnp.float32(0.0)), axis=0)


def along(matrix, volume, which_axis):
    patterns = {1: "ab,nbcd->nacd", 2: "ab,ncbd->ncad", 3: "ab,ncdb->ncda"}
    return jnp.einsum(patterns[which_axis], matrix, volume, precision=lax.Precision.HIGHEST)


def hamiltonian(block, potential, magic_matrix, kinetic_matrix):
    count_here = block.shape[0]
    volume = block.reshape(count_here, G, G, G)
    smooth = volume
    for which_axis in (1, 2, 3):
        smooth = along(magic_matrix, smooth, which_axis)
    smooth = smooth * potential.reshape(1, G, G, G)
    for which_axis in (1, 2, 3):
        smooth = along(magic_matrix.T, smooth, which_axis)
    kinetic_part = (
        along(kinetic_matrix, volume, 1)
        + along(kinetic_matrix, volume, 2)
        + along(kinetic_matrix, volume, 3)
    )
    return (smooth + kinetic_part).reshape(count_here, G * G * G)


def margin_terms(left, right):
    return jnp.einsum("jc,ic->ji", left, right, precision=lax.Precision.HIGHEST) * (1.0 / NC)


def rotate(margin, panel):
    return jnp.einsum("ji,jc->ic", margin, panel, precision=lax.Precision.HIGHEST)


def plain_shards(orbitals, potential, magic_taps, kinetic_taps):
    magic_matrix = filter_matrix(magic_taps, G)
    kinetic_matrix = filter_matrix(kinetic_taps, G)
    hpsi = hamiltonian(orbitals, potential, magic_matrix, kinetic_matrix)
    psi_cols, hpsi_cols = (
        lax.all_to_all(orbitals, "orb", split_axis=1, concat_axis=0, tiled=True),
        lax.all_to_all(hpsi, "orb", split_axis=1, concat_axis=0, tiled=True),
    )
    psi_every = lax.all_gather(psi_cols, "pan", axis=0, tiled=True)
    margin = lax.psum(margin_terms(psi_every, hpsi_cols), "orb")
    grad_cols = hpsi_cols - rotate(margin, psi_every)
    gradient = lax.all_to_all(grad_cols, "orb", split_axis=0, concat_axis=1, tiled=True)
    return gradient


BF = jnp.bfloat16
F32 = jnp.float32
UNIT = 8
CHUNK = UNIT * G
PARTS = G // UNIT
PER = 2


def split(value):
    high = value.astype(BF)
    return high, (value - high.astype(F32)).astype(BF)


def mul(left, right):
    return jnp.dot(left, right, preferred_element_type=F32)


def pick(rows3, matrix, cols):
    first = matrix.astype(BF)
    rest = matrix - first.astype(F32)
    second = rest.astype(BF)
    third = (rest - second.astype(F32)).astype(BF)
    stack = jnp.concatenate([mul(piece, cols).astype(BF) for piece in (first, second, third)], axis=0)
    return mul(rows3, stack)


def one_hot(values, repeat=1):
    hot = (np.asarray(values)[:, None] % G == np.arange(G)[None, :]).astype(np.float32)
    return jnp.asarray(np.concatenate([hot] * repeat, axis=1), dtype=BF)


def block_range(tap_count):
    centre = (tap_count - 1) // 2
    reach = max(centre, tap_count - 1 - centre)
    return -(-reach // UNIT)


def kernel(n, n_pan, own, cols, n_mag, n_kin,
           psi_ref, v_ref, mats_ref, ez3_ref, ezt_ref, ey3_ref, eyt_ref, ex3_ref, ext_ref, same_ref,
           out_ref,
           wfh, wfl, wbh, wbl, wkh, wkl, xl1, xl2, xb1, sh, sl, xs, kx, kyz, tt, vs,
           hbuf, pc, hc, pm_h, pm_l, hm, gbuf, mp, red, mrow, mall,
           psend, precv, hsend, hrecv, rsend, rrecv, bsend, brecv, gsend, grecv, lsem):
    me = lax.axis_index("orb") * n_pan + lax.axis_index("pan")
    total = n * own
    rows = G * own

    def coords(index):
        return {"orb": lax.div(index, n_pan), "pan": lax.rem(index, n_pan)}

    def each(action):
        def step(k, carry):
            action(lax.rem(me + k, n))
            return carry
        lax.fori_loop(1, n, step, 0)

    def sender(src, dst, send, recv):
        def copy(t):
            return pltpu.make_async_remote_copy(
                src_ref=src(t), dst_ref=dst(me), send_sem=send.at[t], recv_sem=recv.at[me],
                device_id=coords(t), device_id_type=pl.DeviceIdType.MESH)

        def arrival(t):
            return pltpu.make_async_remote_copy(
                src_ref=src(t), dst_ref=dst(t), send_sem=send.at[t], recv_sem=recv.at[t],
                device_id=coords(t), device_id_type=pl.DeviceIdType.MESH)
        return (lambda: each(lambda t: copy(t).start()),
                lambda: each(lambda t: arrival(t).wait_recv()),
                lambda: each(lambda t: copy(t).wait_send()))

    def col_slice(ref, t):
        return ref.at[:, pl.ds(pl.multiple_of(t * cols, 128), cols)]

    barrier = pltpu.get_barrier_semaphore()
    each(lambda t: pl.semaphore_signal(barrier, inc=1, device_id=coords(t), device_id_type=pl.DeviceIdType.MESH))
    pl.semaphore_wait(barrier, n - 1)

    p_start, p_arrive, p_sent = sender(lambda t: col_slice(psi_ref, t), lambda t: pc.at[t], psend, precv)
    h_start, h_arrive, h_sent = sender(lambda t: hbuf.at[t], lambda t: hc.at[t], hsend, hrecv)
    r_start, r_arrive, r_sent = sender(lambda t: mp.at[t], lambda t: red.at[t], rsend, rrecv)
    b_start, b_arrive, b_sent = sender(lambda t: mrow, lambda t: mall.at[t], bsend, brecv)
    g_start, g_arrive, g_sent = sender(lambda t: gbuf.at[t], lambda t: col_slice(out_ref, t), gsend, grecv)

    p_start()
    own_psi = pltpu.make_async_copy(col_slice(psi_ref, me), pc.at[me], lsem.at[0])
    own_psi.start()

    fm, fmt, fk, fkt = (mats_ref[i] for i in range(4))
    ez3, ezt = ez3_ref[...], ezt_ref[...]
    eyt = eyt_ref[...]
    halo = max(n_mag, n_kin)
    z_fwd, z_bwd, z_kin = (pick(ez3, m, ezt) for m in (fmt, fm, fkt))
    same_z = mul(ez3[:, :G], ezt)
    same_y = mul(ey3_ref[halo, :, :G], eyt)
    for reach, matrix, z_part, high, low in (
        (n_mag, fmt, z_fwd, wfh, wfl), (n_mag, fm, z_bwd, wbh, wbl), (n_kin, fkt, None, wkh, wkl)):
        for d in range(-reach, reach + 1):
            y_part = pick(ey3_ref[d + halo], matrix, eyt)
            if z_part is not None:
                block = y_part * z_part
            else:
                block = y_part * same_z
                if d == 0:
                    block = block + same_y * z_kin
            at = pl.ds((d + reach) * CHUNK, CHUNK)
            high[at, :], low[at, :] = split(block)
    ex3, ext = ex3_ref[...], ext_ref[...]
    same = same_ref[...]
    mh, ml = split(pick(ex3, fm, ext) * same)
    kh, kl = split(pick(ex3, fk, ext) * same)
    nh, nl = split(pick(ex3, fmt, ext) * same)
    for i, piece in enumerate((mh, ml, kh, kl)):
        xl1[i * rows:(i + 1) * rows, :] = piece
    for i, piece in enumerate((mh, kh)):
        xl2[i * rows:(i + 1) * rows, :] = piece
    for i, piece in enumerate((nh, nl)):
        xb1[i * rows:(i + 1) * rows, :] = piece

    plane = G * G
    for x in range(G):
        xs[x * own:(x + 1) * own, :] = psi_ref[:, x * plane:(x + 1) * plane]

    def fill(c, value):
        high, low = split(value)
        for e in range(PARTS + 2 * halo):
            if (e - halo) % PARTS == c:
                sh[e * rows:(e + 1) * rows, :] = high
                sl[e * rows:(e + 1) * rows, :] = low
        return high, low

    def planes(reach, high, low, finish):
        def step(i, carry):
            def left(ref):
                return jnp.concatenate(
                    [ref[pl.ds(pl.multiple_of((i * PER + d + halo) * rows, 16), PER * rows), :]
                     for d in range(-reach, reach + 1)], axis=1)
            left_h, left_l = left(sh), left(sl)
            value = mul(left_h, high[...]) + mul(left_h, low[...]) + mul(left_l, high[...])
            finish(pl.ds(pl.multiple_of(i * PER * rows, 8), PER * rows), value)
            return carry
        lax.fori_loop(0, PARTS // PER, step, 0)

    def put(ref):
        def finish(at, value):
            ref[at, :] = value
        return finish

    v_first = v_ref[...].astype(BF)
    v_rest = v_ref[...] - v_first.astype(F32)
    v_second = v_rest.astype(BF)
    v_third = (v_rest - v_second.astype(F32)).astype(BF)
    v_stack = jnp.concatenate([v_first, v_second, v_third], axis=0)
    for c in range(PARTS):
        lanes = slice(c * CHUNK, (c + 1) * CHUNK)
        vs[c * rows:(c + 1) * rows, :] = mul(ex3, v_stack[:, lanes])
        fill(c, xs[:, lanes])
    planes(n_kin, wkh, wkl, put(kyz))
    for c in range(PARTS):
        high, low = split(xs[:, c * CHUNK:(c + 1) * CHUNK])
        one = mul(xl1[...], high)
        two = mul(xl2[...], low)
        fill(c, one[:rows] + one[rows:2 * rows] + two[:rows])
        kx[c * rows:(c + 1) * rows, :] = one[2 * rows:3 * rows] + one[3 * rows:] + two[rows:]

    def with_potential(at, value):
        tt[at, :] = value * vs[at, :]
    planes(n_mag, wfh, wfl, with_potential)
    for c in range(PARTS):
        fill(c, tt[c * rows:(c + 1) * rows, :])
    planes(n_mag, wbh, wbl, put(tt))
    for c in range(PARTS):
        at = slice(c * rows, (c + 1) * rows)
        high, low = split(tt[at, :])
        one = mul(xb1[...], high)
        xs[:, c * CHUNK:(c + 1) * CHUNK] = (
            one[:rows] + one[rows:] + mul(xb1[:rows, :], low) + kx[at, :] + kyz[at, :])
    for x in range(G):
        at, stop = x * plane, (x + 1) * plane
        while at < stop:
            d = at // cols
            until = min(stop, (d + 1) * cols)
            hbuf[d, :, at - d * cols:until - d * cols] = xs[
                x * own:(x + 1) * own, at - x * plane:until - x * plane]
            at = until

    h_start()
    own_h = pltpu.make_async_copy(hbuf.at[me], hc.at[me], lsem.at[1])
    own_h.start()

    own_psi.wait()
    p_arrive()
    for t in range(n):
        hm[t * own:(t + 1) * own, :] = pc[t]
    pm_h[...], pm_l[...] = split(hm[...])

    own_h.wait()
    h_arrive()
    for t in range(n):
        hm[t * own:(t + 1) * own, :] = hc[t]
    h_high, h_low = split(hm[...])
    nt = (((1,), (1,)), ((), ()))

    def mul_t(left, right):
        return lax.dot_general(left, right, nt, preferred_element_type=F32)
    part = (mul_t(h_high, pm_h[...]) + mul_t(h_high, pm_l[...]) + mul_t(h_low, pm_h[...])) * (1.0 / NC)
    for t in range(n):
        mp[t] = part[t * own:(t + 1) * own, :]

    r_start()
    own_m = pltpu.make_async_copy(mp.at[me], red.at[me], lsem.at[2])
    own_m.start()
    own_m.wait()
    r_arrive()
    mrow[...] = jnp.sum(red[...], axis=0)
    b_start()
    own_r = pltpu.make_async_copy(mrow, mall.at[me], lsem.at[3])
    own_r.start()
    own_r.wait()
    b_arrive()
    margin_t = jnp.concatenate([mall[t] for t in range(n)], axis=0)
    m_high, m_low = split(margin_t)
    hm[...] = hm[...] - (mul(m_high, pm_h[...]) + mul(m_high, pm_l[...]) + mul(m_low, pm_h[...]))
    for t in range(n):
        gbuf[t] = hm[t * own:(t + 1) * own, :]
    g_start()
    own_g = pltpu.make_async_copy(gbuf.at[me], col_slice(out_ref, me), lsem.at[4])
    own_g.start()
    own_g.wait()
    p_sent()
    h_sent()
    r_sent()
    b_sent()
    g_arrive()
    g_sent()


def shards(n, n_pan, orbitals, potential, magic_taps, kinetic_taps):
    own, width = orbitals.shape
    cols = width // n
    rows, total = G * own, n * own
    magic_matrix = filter_matrix(magic_taps, G)
    kinetic_matrix = filter_matrix(kinetic_taps, G)
    mats = jnp.stack([magic_matrix, magic_matrix.T, kinetic_matrix, kinetic_matrix.T])
    n_mag, n_kin = block_range(magic_taps.shape[0]), block_range(kinetic_taps.shape[0])
    halo = max(n_mag, n_kin)
    lane = np.arange(CHUNK)
    ez3, ezt = one_hot(lane, 3), one_hot(lane).T
    ey3 = jnp.stack([one_hot(lane // G + UNIT * d, 3) for d in range(-halo, halo + 1)])
    eyt = one_hot(lane // G).T
    row = np.arange(rows)
    ex3, ext = one_hot(row // own, 3), one_hot(row // own).T
    same = jnp.asarray((row[:, None] % own == row[None, :] % own).astype(np.float32))
    vmem = pl.BlockSpec(memory_space=pltpu.VMEM)
    span_m, span_k = (2 * n_mag + 1) * CHUNK, (2 * n_kin + 1) * CHUNK
    chunked = pltpu.VMEM((PARTS * rows, CHUNK), F32)
    halved = pltpu.VMEM(((PARTS + 2 * halo) * rows, CHUNK), BF)
    blocks = pltpu.VMEM((n, own, cols), F32)
    dma = pltpu.SemaphoreType.DMA
    return pl.pallas_call(
        functools.partial(kernel, n, n_pan, own, cols, n_mag, n_kin),
        out_shape=jax.ShapeDtypeStruct((own, width), F32),
        in_specs=[vmem] * 10,
        out_specs=pl.BlockSpec(memory_space=OUT_SPACE),
        scratch_shapes=[
            pltpu.VMEM((span_m, CHUNK), BF), pltpu.VMEM((span_m, CHUNK), BF),
            pltpu.VMEM((span_m, CHUNK), BF), pltpu.VMEM((span_m, CHUNK), BF),
            pltpu.VMEM((span_k, CHUNK), BF), pltpu.VMEM((span_k, CHUNK), BF),
            pltpu.VMEM((4 * rows, rows), BF), pltpu.VMEM((2 * rows, rows), BF), pltpu.VMEM((2 * rows, rows), BF),
            halved, halved,
            pltpu.VMEM((rows, G * G), F32), chunked, chunked, chunked, chunked,
            blocks, blocks, blocks,
            pltpu.VMEM((total, cols), BF), pltpu.VMEM((total, cols), BF), pltpu.VMEM((total, cols), F32),
            blocks,
            pltpu.VMEM((n, own, total), F32), pltpu.VMEM((n, own, total), F32),
            pltpu.VMEM((own, total), F32), pltpu.VMEM((n, own, total), F32),
            dma((n,)), dma((n,)), dma((n,)), dma((n,)), dma((n,)), dma((n,)), dma((n,)), dma((n,)),
            dma((n,)), dma((n,)), dma((5,)),
        ],
        compiler_params=pltpu.CompilerParams(
            collective_id=0, has_side_effects=True, vmem_limit_bytes=60 * 1024 * 1024),
    )(orbitals, potential.reshape(G, G * G), mats, ez3, ezt, ey3, eyt, ex3, ext, same)


OUT_SPACE = pl.ANY


def solution(mesh):
    placed = (P(("orb", "pan"), None), P(), P(), P())
    n_pan = mesh.shape["pan"]
    n = mesh.shape["orb"] * n_pan
    aligned = NC % (n * 128) == 0
    body = functools.partial(shards, n, n_pan) if aligned else plain_shards
    return jax.shard_map(
        body, mesh=mesh, in_specs=placed, out_specs=P(("orb", "pan"), None), check_vma=False
    )
```

```python
import functools

import jax
import jax.numpy as jnp
import numpy as np
from jax import lax
from jax.experimental import pallas as pl
from jax.experimental.pallas import tpu as pltpu
from jax.sharding import PartitionSpec as P

G = 48
NC = 110592


def filter_matrix(tap_values, extent):
    tap_count = tap_values.shape[0]
    centre = (tap_count - 1) // 2
    tap_ids = lax.broadcasted_iota(jnp.int32, (tap_count, extent, extent), 0)
    row_ids = lax.broadcasted_iota(jnp.int32, (tap_count, extent, extent), 1)
    col_ids = lax.broadcasted_iota(jnp.int32, (tap_count, extent, extent), 2)
    offset = (col_ids - row_ids - (tap_ids - centre)) % extent
    return jnp.sum(jnp.where(offset == 0, tap_values[:, None, None], jnp.float32(0.0)), axis=0)


def along(matrix, volume, which_axis):
    patterns = {1: "ab,nbcd->nacd", 2: "ab,ncbd->ncad", 3: "ab,ncdb->ncda"}
    return jnp.einsum(patterns[which_axis], matrix, volume, precision=lax.Precision.HIGHEST)


def hamiltonian(block, potential, magic_matrix, kinetic_matrix):
    count_here = block.shape[0]
    volume = block.reshape(count_here, G, G, G)
    smooth = volume
    for which_axis in (1, 2, 3):
        smooth = along(magic_matrix, smooth, which_axis)
    smooth = smooth * potential.reshape(1, G, G, G)
    for which_axis in (1, 2, 3):
        smooth = along(magic_matrix.T, smooth, which_axis)
    kinetic_part = (
        along(kinetic_matrix, volume, 1)
        + along(kinetic_matrix, volume, 2)
        + along(kinetic_matrix, volume, 3)
    )
    return (smooth + kinetic_part).reshape(count_here, G * G * G)


def margin_terms(left, right):
    return jnp.einsum("jc,ic->ji", left, right, precision=lax.Precision.HIGHEST) * (1.0 / NC)


def rotate(margin, panel):
    return jnp.einsum("ji,jc->ic", margin, panel, precision=lax.Precision.HIGHEST)


def plain_shards(orbitals, potential, magic_taps, kinetic_taps):
    magic_matrix = filter_matrix(magic_taps, G)
    kinetic_matrix = filter_matrix(kinetic_taps, G)
    hpsi = hamiltonian(orbitals, potential, magic_matrix, kinetic_matrix)
    psi_cols, hpsi_cols = (
        lax.all_to_all(orbitals, "orb", split_axis=1, concat_axis=0, tiled=True),
        lax.all_to_all(hpsi, "orb", split_axis=1, concat_axis=0, tiled=True),
    )
    psi_every = lax.all_gather(psi_cols, "pan", axis=0, tiled=True)
    margin = lax.psum(margin_terms(psi_every, hpsi_cols), "orb")
    grad_cols = hpsi_cols - rotate(margin, psi_every)
    gradient = lax.all_to_all(grad_cols, "orb", split_axis=0, concat_axis=1, tiled=True)
    return gradient


BF = jnp.bfloat16
F32 = jnp.float32
UNIT = 8
CHUNK = UNIT * G
PARTS = G // UNIT
PER = 2


def split(value):
    high = value.astype(BF)
    return high, (value - high.astype(F32)).astype(BF)


def mul(left, right):
    return jnp.dot(left, right, preferred_element_type=F32)


def pick(rows3, matrix, cols):
    first = matrix.astype(BF)
    rest = matrix - first.astype(F32)
    second = rest.astype(BF)
    third = (rest - second.astype(F32)).astype(BF)
    stack = jnp.concatenate([mul(piece, cols).astype(BF) for piece in (first, second, third)], axis=0)
    return mul(rows3, stack)


def one_hot(values, repeat=1):
    hot = (np.asarray(values)[:, None] % G == np.arange(G)[None, :]).astype(np.float32)
    return jnp.asarray(np.concatenate([hot] * repeat, axis=1), dtype=BF)


def block_range(tap_count):
    centre = (tap_count - 1) // 2
    reach = max(centre, tap_count - 1 - centre)
    return -(-reach // UNIT)


def filter_of(tap_ref, tap_count, flip):
    centre = (tap_count - 1) // 2
    row_ids = lax.broadcasted_iota(jnp.int32, (G, G), 0)
    col_ids = lax.broadcasted_iota(jnp.int32, (G, G), 1)
    offset = row_ids - col_ids if flip else col_ids - row_ids
    total = jnp.zeros((G, G), F32)
    for k in range(tap_count):
        shift = (k - centre) % G
        hit = (offset == shift) | (offset == shift - G)
        total = total + jnp.where(hit, tap_ref[k], 0.0)
    return total


def kernel(n_orb, n_pan, own, cols, n_mag, n_kin,
           psi_ref, v_ref, mag_ref, kin_ref, ez3_ref, ezt_ref, ey3_ref, eyt_ref, ex3_ref, ext_ref, same_ref,
           out_ref,
           wfh, wfl, wbh, wbl, wkh, wkl, xl1, xl2, xb1, sh, sl, xs, kx, kyz, tt, vs, vrows,
           hbuf, pc, hc, pm_h, pm_l, pf, hm, gbuf, mp, red, mrow, mall,
           psend, precv, hsend, hrecv, rsend, rrecv, bsend, brecv, gsend, grecv, lsem):
    half = n_pan // 2
    n, n_half = n_orb * n_pan, n_orb * half
    orb, pan = lax.axis_index("orb"), lax.axis_index("pan")
    side = lax.div(pan, half)
    me = orb * n_pan + pan
    member = orb * half + lax.rem(pan, half)
    total = n * own
    rows = G * own

    def at_all(t):
        return {"orb": lax.div(t, n_pan), "pan": lax.rem(t, n_pan)}

    def at_half(t):
        return {"orb": lax.div(t, half), "pan": side * half + lax.rem(t, half)}

    def block_of(t):
        return lax.div(t, n_pan) * half + lax.rem(lax.rem(t, n_pan), half)

    def each(action, count=n, first=me):
        def step(k, carry):
            action(lax.rem(first + k, count))
            return carry
        lax.fori_loop(1, count, step, 0)

    def sender(src, dst, send, recv, count=n_half, mine=member, coords=at_half):
        def copy(t):
            return pltpu.make_async_remote_copy(
                src_ref=src(t), dst_ref=dst(mine), send_sem=send.at[t], recv_sem=recv.at[mine],
                device_id=coords(t), device_id_type=pl.DeviceIdType.MESH)

        def arrival(t):
            return pltpu.make_async_remote_copy(
                src_ref=src(t), dst_ref=dst(t), send_sem=send.at[t], recv_sem=recv.at[t],
                device_id=coords(t), device_id_type=pl.DeviceIdType.MESH)
        return (lambda: each(lambda t: copy(t).start(), count, mine),
                lambda: each(lambda t: arrival(t).wait_recv(), count, mine),
                lambda: each(lambda t: copy(t).wait_send(), count, mine))

    def col_slice(ref, block):
        return ref.at[:, pl.ds(pl.multiple_of(block * cols, 128), cols)]

    barrier = pltpu.get_barrier_semaphore()
    each(lambda t: pl.semaphore_signal(barrier, inc=1, device_id=at_all(t), device_id_type=pl.DeviceIdType.MESH))
    pl.semaphore_wait(barrier, n - 1)

    p_start, p_arrive, p_sent = sender(
        lambda t: col_slice(psi_ref, block_of(t)), lambda t: pc.at[t], psend, precv, n, me, at_all)
    h_start, h_arrive, h_sent = sender(lambda t: hbuf.at[t], lambda t: hc.at[t], hsend, hrecv)
    r_start, r_arrive, r_sent = sender(lambda t: mp.at[t], lambda t: red.at[t], rsend, rrecv)
    b_start, b_arrive, b_sent = sender(lambda t: mrow, lambda t: mall.at[t], bsend, brecv)
    g_start, g_arrive, g_sent = sender(lambda t: gbuf.at[t], lambda t: col_slice(out_ref, t), gsend, grecv)

    p_start()
    own_psi = pltpu.make_async_copy(col_slice(psi_ref, member), pc.at[me], lsem.at[0])
    own_psi.start()

    fm, fmt = (filter_of(mag_ref, mag_ref.shape[0], flip) for flip in (False, True))
    fk, fkt = (filter_of(kin_ref, kin_ref.shape[0], flip) for flip in (False, True))
    ez3, ezt = ez3_ref[...], ezt_ref[...]
    eyt = eyt_ref[...]
    halo = max(n_mag, n_kin)
    z_fwd, z_bwd, z_kin = (pick(ez3, m, ezt) for m in (fmt, fm, fkt))
    same_z = mul(ez3[:, :G], ezt)
    same_y = mul(ey3_ref[halo, :, :G], eyt)
    for reach, matrix, z_part, high, low in (
        (n_mag, fmt, z_fwd, wfh, wfl), (n_mag, fm, z_bwd, wbh, wbl), (n_kin, fkt, None, wkh, wkl)):
        for d in range(-reach, reach + 1):
            y_part = pick(ey3_ref[d + halo], matrix, eyt)
            if z_part is not None:
                block = y_part * z_part
            else:
                block = y_part * same_z
                if d == 0:
                    block = block + same_y * z_kin
            at = pl.ds((d + reach) * CHUNK, CHUNK)
            high[at, :], low[at, :] = split(block)
    ex3, ext = ex3_ref[...], ext_ref[...]
    same = same_ref[...]
    mh, ml = split(pick(ex3, fm, ext) * same)
    kh, kl = split(pick(ex3, fk, ext) * same)
    nh, nl = split(pick(ex3, fmt, ext) * same)
    for i, piece in enumerate((mh, ml, kh, kl)):
        xl1[i * rows:(i + 1) * rows, :] = piece
    for i, piece in enumerate((mh, kh)):
        xl2[i * rows:(i + 1) * rows, :] = piece
    for i, piece in enumerate((nh, nl)):
        xb1[i * rows:(i + 1) * rows, :] = piece

    plane = G * G
    for x in range(G):
        xs[x * own:(x + 1) * own, :] = psi_ref[:, x * plane:(x + 1) * plane]
        vrows[x:x + 1, :] = v_ref[:, x * plane:(x + 1) * plane]

    def fill(c, value):
        high, low = split(value)
        for e in range(PARTS + 2 * halo):
            if (e - halo) % PARTS == c:
                sh[e * rows:(e + 1) * rows, :] = high
                sl[e * rows:(e + 1) * rows, :] = low
        return high, low

    def planes(reach, high, low, finish):
        def step(i, carry):
            def left(ref):
                return jnp.concatenate(
                    [ref[pl.ds(pl.multiple_of((i * PER + d + halo) * rows, 16), PER * rows), :]
                     for d in range(-reach, reach + 1)], axis=1)
            left_h, left_l = left(sh), left(sl)
            value = mul(left_h, high[...]) + mul(left_h, low[...]) + mul(left_l, high[...])
            finish(pl.ds(pl.multiple_of(i * PER * rows, 8), PER * rows), value)
            return carry
        lax.fori_loop(0, PARTS // PER, step, 0)

    def put(ref):
        def finish(at, value):
            ref[at, :] = value
        return finish

    v_first = vrows[...].astype(BF)
    v_rest = vrows[...] - v_first.astype(F32)
    v_second = v_rest.astype(BF)
    v_third = (v_rest - v_second.astype(F32)).astype(BF)
    v_stack = jnp.concatenate([v_first, v_second, v_third], axis=0)
    for c in range(PARTS):
        lanes = slice(c * CHUNK, (c + 1) * CHUNK)
        vs[c * rows:(c + 1) * rows, :] = mul(ex3, v_stack[:, lanes])
        fill(c, xs[:, lanes])
    planes(n_kin, wkh, wkl, put(kyz))
    for c in range(PARTS):
        high, low = split(xs[:, c * CHUNK:(c + 1) * CHUNK])
        one = mul(xl1[...], high)
        two = mul(xl2[...], low)
        fill(c, one[:rows] + one[rows:2 * rows] + two[:rows])
        kx[c * rows:(c + 1) * rows, :] = one[2 * rows:3 * rows] + one[3 * rows:] + two[rows:]

    def with_potential(at, value):
        tt[at, :] = value * vs[at, :]
    planes(n_mag, wfh, wfl, with_potential)
    for c in range(PARTS):
        fill(c, tt[c * rows:(c + 1) * rows, :])
    planes(n_mag, wbh, wbl, put(tt))
    for c in range(PARTS):
        at = slice(c * rows, (c + 1) * rows)
        high, low = split(tt[at, :])
        one = mul(xb1[...], high)
        xs[:, c * CHUNK:(c + 1) * CHUNK] = (
            one[:rows] + one[rows:] + mul(xb1[:rows, :], low) + kx[at, :] + kyz[at, :])
    for x in range(G):
        at, stop = x * plane, (x + 1) * plane
        while at < stop:
            d = at // cols
            until = min(stop, (d + 1) * cols)
            hbuf[d, :, at - d * cols:until - d * cols] = xs[
                x * own:(x + 1) * own, at - x * plane:until - x * plane]
            at = until

    h_start()
    own_h = pltpu.make_async_copy(hbuf.at[member], hc.at[member], lsem.at[1])
    own_h.start()

    own_psi.wait()
    p_arrive()
    for t in range(n):
        pf[t * own:(t + 1) * own, :] = pc[t]
    pm_h[...], pm_l[...] = split(pf[...])

    own_h.wait()
    h_arrive()
    for t in range(n_half):
        hm[t * own:(t + 1) * own, :] = hc[t]
    h_high, h_low = split(hm[...])
    nt = (((1,), (1,)), ((), ()))

    def mul_t(left, right):
        return lax.dot_general(left, right, nt, preferred_element_type=F32)
    part = (mul_t(h_high, pm_h[...]) + mul_t(h_high, pm_l[...]) + mul_t(h_low, pm_h[...])) * (1.0 / NC)
    for t in range(n_half):
        mp[t] = part[t * own:(t + 1) * own, :]

    r_start()
    own_m = pltpu.make_async_copy(mp.at[member], red.at[member], lsem.at[2])
    own_m.start()
    own_m.wait()
    r_arrive()
    mrow[...] = jnp.sum(red[...], axis=0)
    b_start()
    own_r = pltpu.make_async_copy(mrow, mall.at[member], lsem.at[3])
    own_r.start()
    own_r.wait()
    b_arrive()
    margin_t = jnp.concatenate([mall[t] for t in range(n_half)], axis=0)
    m_high, m_low = split(margin_t)
    hm[...] = hm[...] - (mul(m_high, pm_h[...]) + mul(m_high, pm_l[...]) + mul(m_low, pm_h[...]))
    for t in range(n_half):
        gbuf[t] = hm[t * own:(t + 1) * own, :]
    g_start()
    own_g = pltpu.make_async_copy(gbuf.at[member], col_slice(out_ref, member), lsem.at[4])
    own_g.start()
    own_g.wait()
    p_sent()
    h_sent()
    r_sent()
    b_sent()
    g_arrive()
    g_sent()


def shards(n_orb, n_pan, orbitals, potential, magic_taps, kinetic_taps):
    own, width = orbitals.shape
    n, n_half = n_orb * n_pan, n_orb * (n_pan // 2)
    cols = width // n_half
    rows, total = G * own, n * own
    n_mag, n_kin = block_range(magic_taps.shape[0]), block_range(kinetic_taps.shape[0])
    halo = max(n_mag, n_kin)
    lane = np.arange(CHUNK)
    ez3, ezt = one_hot(lane, 3), one_hot(lane).T
    ey3 = jnp.stack([one_hot(lane // G + UNIT * d, 3) for d in range(-halo, halo + 1)])
    eyt = one_hot(lane // G).T
    row = np.arange(rows)
    ex3, ext = one_hot(row // own, 3), one_hot(row // own).T
    same = jnp.asarray((row[:, None] % own == row[None, :] % own).astype(np.float32))
    vmem = pl.BlockSpec(memory_space=pltpu.VMEM)
    span_m, span_k = (2 * n_mag + 1) * CHUNK, (2 * n_kin + 1) * CHUNK
    chunked = pltpu.VMEM((PARTS * rows, CHUNK), F32)
    halved = pltpu.VMEM(((PARTS + 2 * halo) * rows, CHUNK), BF)
    smem = pl.BlockSpec(memory_space=pltpu.SMEM)
    blocks = pltpu.VMEM((n_half, own, cols), F32)
    dma = pltpu.SemaphoreType.DMA
    return pl.pallas_call(
        functools.partial(kernel, n_orb, n_pan, own, cols, n_mag, n_kin),
        out_shape=jax.ShapeDtypeStruct((own, width), F32),
        in_specs=[vmem] * 2 + [smem] * 2 + [vmem] * 7,
        out_specs=pl.BlockSpec(memory_space=OUT_SPACE),
        scratch_shapes=[
            pltpu.VMEM((span_m, CHUNK), BF), pltpu.VMEM((span_m, CHUNK), BF),
            pltpu.VMEM((span_m, CHUNK), BF), pltpu.VMEM((span_m, CHUNK), BF),
            pltpu.VMEM((span_k, CHUNK), BF), pltpu.VMEM((span_k, CHUNK), BF),
            pltpu.VMEM((4 * rows, rows), BF), pltpu.VMEM((2 * rows, rows), BF), pltpu.VMEM((2 * rows, rows), BF),
            halved, halved,
            pltpu.VMEM((rows, G * G), F32), chunked, chunked, chunked, chunked,
            pltpu.VMEM((G, G * G), F32),
            blocks, pltpu.VMEM((n, own, cols), F32), blocks,
            pltpu.VMEM((total, cols), BF), pltpu.VMEM((total, cols), BF), pltpu.VMEM((total, cols), F32),
            pltpu.VMEM((n_half * own, cols), F32),
            blocks,
            pltpu.VMEM((n_half, own, total), F32), pltpu.VMEM((n_half, own, total), F32),
            pltpu.VMEM((own, total), F32), pltpu.VMEM((n_half, own, total), F32),
            dma((n,)), dma((n,)), dma((n_half,)), dma((n_half,)), dma((n_half,)), dma((n_half,)), dma((n_half,)),
            dma((n_half,)), dma((n_half,)), dma((n_half,)), dma((5,)),
        ],
        compiler_params=pltpu.CompilerParams(
            collective_id=0, has_side_effects=True, vmem_limit_bytes=60 * 1024 * 1024),
    )(orbitals, potential.reshape(1, width), magic_taps, kinetic_taps, ez3, ezt, ey3, eyt, ex3, ext, same)


OUT_SPACE = pl.ANY


def solution(mesh):
    placed = (P(("orb", "pan"), None), P(), P(), P())
    n_pan = mesh.shape["pan"]
    n_orb = mesh.shape["orb"]
    aligned = n_pan % 2 == 0 and NC % (n_orb * (n_pan // 2) * 128) == 0
    body = functools.partial(shards, n_orb, n_pan) if aligned else plain_shards
    return jax.shard_map(
        body, mesh=mesh, in_specs=placed, out_specs=P(("orb", "pan"), None), check_vma=False
    )
```

```python
import functools
import math

import jax
import jax.numpy as jnp
import numpy as np
from jax import lax
from jax.experimental import pallas as pl
from jax.experimental.pallas import tpu as pltpu
from jax.sharding import PartitionSpec as P

G = 48
NC = 110592


def filter_matrix(tap_values, extent):
    tap_count = tap_values.shape[0]
    centre = (tap_count - 1) // 2
    tap_ids = lax.broadcasted_iota(jnp.int32, (tap_count, extent, extent), 0)
    row_ids = lax.broadcasted_iota(jnp.int32, (tap_count, extent, extent), 1)
    col_ids = lax.broadcasted_iota(jnp.int32, (tap_count, extent, extent), 2)
    offset = (col_ids - row_ids - (tap_ids - centre)) % extent
    return jnp.sum(jnp.where(offset == 0, tap_values[:, None, None], jnp.float32(0.0)), axis=0)


def along(matrix, volume, which_axis):
    patterns = {1: "ab,nbcd->nacd", 2: "ab,ncbd->ncad", 3: "ab,ncdb->ncda"}
    return jnp.einsum(patterns[which_axis], matrix, volume, precision=lax.Precision.HIGHEST)


def hamiltonian(block, potential, magic_matrix, kinetic_matrix):
    count_here = block.shape[0]
    volume = block.reshape(count_here, G, G, G)
    smooth = volume
    for which_axis in (1, 2, 3):
        smooth = along(magic_matrix, smooth, which_axis)
    smooth = smooth * potential.reshape(1, G, G, G)
    for which_axis in (1, 2, 3):
        smooth = along(magic_matrix.T, smooth, which_axis)
    kinetic_part = (
        along(kinetic_matrix, volume, 1)
        + along(kinetic_matrix, volume, 2)
        + along(kinetic_matrix, volume, 3)
    )
    return (smooth + kinetic_part).reshape(count_here, G * G * G)


def margin_terms(left, right):
    return jnp.einsum("jc,ic->ji", left, right, precision=lax.Precision.HIGHEST) * (1.0 / NC)


def rotate(margin, panel):
    return jnp.einsum("ji,jc->ic", margin, panel, precision=lax.Precision.HIGHEST)


def plain_shards(orbitals, potential, magic_taps, kinetic_taps):
    magic_matrix = filter_matrix(magic_taps, G)
    kinetic_matrix = filter_matrix(kinetic_taps, G)
    hpsi = hamiltonian(orbitals, potential, magic_matrix, kinetic_matrix)
    psi_cols, hpsi_cols = (
        lax.all_to_all(orbitals, "orb", split_axis=1, concat_axis=0, tiled=True),
        lax.all_to_all(hpsi, "orb", split_axis=1, concat_axis=0, tiled=True),
    )
    psi_every = lax.all_gather(psi_cols, "pan", axis=0, tiled=True)
    margin = lax.psum(margin_terms(psi_every, hpsi_cols), "orb")
    grad_cols = hpsi_cols - rotate(margin, psi_every)
    gradient = lax.all_to_all(grad_cols, "orb", split_axis=0, concat_axis=1, tiled=True)
    return gradient


BF = jnp.bfloat16
F32 = jnp.float32
UNIT = 8
CHUNK = UNIT * G
PARTS = G // UNIT
PER = 2


def split(value):
    high = value.astype(BF)
    return high, (value - high.astype(F32)).astype(BF)


def mul(left, right):
    return jnp.dot(left, right, preferred_element_type=F32)


def pick(rows3, matrix, cols):
    first = matrix.astype(BF)
    rest = matrix - first.astype(F32)
    second = rest.astype(BF)
    third = (rest - second.astype(F32)).astype(BF)
    stack = jnp.concatenate([mul(piece, cols).astype(BF) for piece in (first, second, third)], axis=0)
    return mul(rows3, stack)


def one_hot(values, repeat=1):
    hot = (np.asarray(values)[:, None] % G == np.arange(G)[None, :]).astype(np.float32)
    return jnp.asarray(np.concatenate([hot] * repeat, axis=1), dtype=BF)


def block_range(tap_count):
    centre = (tap_count - 1) // 2
    reach = max(centre, tap_count - 1 - centre)
    return -(-reach // UNIT)


def filter_of(tap_ref, tap_count, flip):
    centre = (tap_count - 1) // 2
    row_ids = lax.broadcasted_iota(jnp.int32, (G, G), 0)
    col_ids = lax.broadcasted_iota(jnp.int32, (G, G), 1)
    offset = row_ids - col_ids if flip else col_ids - row_ids
    total = jnp.zeros((G, G), F32)
    for k in range(tap_count):
        shift = (k - centre) % G
        hit = (offset == shift) | (offset == shift - G)
        total = total + jnp.where(hit, tap_ref[k], 0.0)
    return total


def kernel(n_orb, n_pan, own, cols, n_mag, n_kin, pieces, per_tile,
           psi_ref, v_ref, mag_ref, kin_ref, ez3_ref, ezt_ref, ey3_ref, eyt_ref, ex3_ref, ext_ref, same_ref,
           out_ref,
           wfh, wfl, wbh, wbl, wkh, wkl, xl1, xl2, xb1, sh, sl, xs, kx, kyz, tt, vs, vrows,
           psi_vm, hbuf, pc, hc, pm_h, pm_l, pf, hm, hs, gbuf, mp, red, mrow, mall,
           psend, precv, hsend, hrecv, rsend, rrecv, bsend, brecv, gsend, grecv, lsem):
    half = n_pan // 2
    n, n_half = n_orb * n_pan, n_orb * half
    orb, pan = lax.axis_index("orb"), lax.axis_index("pan")
    side = lax.div(pan, half)
    me = orb * n_pan + pan
    member = orb * half + lax.rem(pan, half)
    total = n * own
    rows = G * own

    def at_all(t):
        return {"orb": lax.div(t, n_pan), "pan": lax.rem(t, n_pan)}

    def at_half(t):
        return {"orb": lax.div(t, half), "pan": side * half + lax.rem(t, half)}

    def block_of(t):
        return lax.div(t, n_pan) * half + lax.rem(lax.rem(t, n_pan), half)

    def each(action, count=n, first=me):
        for k in range(1, count):
            action(lax.rem(first + k, count))

    def sender(src, dst, send, recv, count=n_half, mine=member, coords=at_half):
        def copy(t):
            return pltpu.make_async_remote_copy(
                src_ref=src(t), dst_ref=dst(mine), send_sem=send.at[t], recv_sem=recv.at[mine],
                device_id=coords(t), device_id_type=pl.DeviceIdType.MESH)

        def arrival(t):
            return pltpu.make_async_remote_copy(
                src_ref=src(t), dst_ref=dst(t), send_sem=send.at[t], recv_sem=recv.at[t],
                device_id=coords(t), device_id_type=pl.DeviceIdType.MESH)
        return (lambda: each(lambda t: copy(t).start(), count, mine),
                lambda: each(lambda t: arrival(t).wait_recv(), count, mine),
                lambda: each(lambda t: copy(t).wait_send(), count, mine))

    def col_slice(ref, block):
        return ref.at[:, pl.ds(pl.multiple_of(block * cols, 128), cols)]

    load = pltpu.make_async_copy(psi_ref, psi_vm, lsem.at[0])
    load.start()
    barrier = pltpu.get_barrier_semaphore()
    each(lambda t: pl.semaphore_signal(barrier, inc=1, device_id=at_all(t), device_id_type=pl.DeviceIdType.MESH))
    pl.semaphore_wait(barrier, n - 1)

    def psi_copy(k):
        t = lax.rem(me + k, n)
        return pltpu.make_async_remote_copy(
            src_ref=col_slice(psi_ref, block_of(t)), dst_ref=pc.at[n - k], send_sem=psend.at[k],
            recv_sem=precv.at[n - k], device_id=at_all(t), device_id_type=pl.DeviceIdType.MESH)

    def p_start():
        for k in range(1, n):
            psi_copy(k).start()

    def p_sent():
        for k in range(1, n):
            psi_copy(k).wait_send()
    h_start, h_arrive, h_sent = sender(lambda t: hbuf.at[t], lambda t: hc.at[t], hsend, hrecv)
    r_start, r_arrive, r_sent = sender(lambda t: mp.at[t], lambda t: red.at[t], rsend, rrecv)
    b_start, b_arrive, b_sent = sender(lambda t: mrow, lambda t: mall.at[t], bsend, brecv)
    wide = cols // pieces
    g_pieces = [
        sender(lambda t, c=c: gbuf.at[c, t],
               lambda t, c=c: out_ref.at[:, pl.ds(pl.multiple_of(t * cols + c * wide, 128), wide)],
               gsend.at[c], grecv.at[c]) for c in range(pieces)]

    p_start()
    load.wait()
    pc[0] = psi_vm[:, pl.ds(pl.multiple_of(member * cols, 128), cols)]

    fm, fmt = (filter_of(mag_ref, mag_ref.shape[0], flip) for flip in (False, True))
    fk, fkt = (filter_of(kin_ref, kin_ref.shape[0], flip) for flip in (False, True))
    ez3, ezt = ez3_ref[...], ezt_ref[...]
    eyt = eyt_ref[...]
    halo = max(n_mag, n_kin)
    z_fwd, z_bwd, z_kin = (pick(ez3, m, ezt) for m in (fmt, fm, fkt))
    same_z = mul(ez3[:, :G], ezt)
    same_y = mul(ey3_ref[halo, :, :G], eyt)
    for reach, matrix, z_part, high, low in (
        (n_mag, fmt, z_fwd, wfh, wfl), (n_mag, fm, z_bwd, wbh, wbl), (n_kin, fkt, None, wkh, wkl)):
        for d in range(-reach, reach + 1):
            y_part = pick(ey3_ref[d + halo], matrix, eyt)
            if z_part is not None:
                block = y_part * z_part
            else:
                block = y_part * same_z
                if d == 0:
                    block = block + same_y * z_kin
            at = pl.ds((d + reach) * CHUNK, CHUNK)
            high[at, :], low[at, :] = split(block)
    ex3, ext = ex3_ref[...], ext_ref[...]
    same = same_ref[...]
    mh, ml = split(pick(ex3, fm, ext) * same)
    kh, kl = split(pick(ex3, fk, ext) * same)
    nh, nl = split(pick(ex3, fmt, ext) * same)
    for i, piece in enumerate((mh, ml, kh, kl)):
        xl1[i * rows:(i + 1) * rows, :] = piece
    for i, piece in enumerate((mh, kh)):
        xl2[i * rows:(i + 1) * rows, :] = piece
    for i, piece in enumerate((nh, nl)):
        xb1[i * rows:(i + 1) * rows, :] = piece

    plane = G * G
    for x in range(G):
        xs[x * own:(x + 1) * own, :] = psi_vm[:, x * plane:(x + 1) * plane]
        vrows[x:x + 1, :] = v_ref[:, x * plane:(x + 1) * plane]

    def fill(c, value):
        high, low = split(value)
        for e in range(PARTS + 2 * halo):
            if (e - halo) % PARTS == c:
                sh[e * rows:(e + 1) * rows, :] = high
                sl[e * rows:(e + 1) * rows, :] = low
        return high, low

    def planes(reach, high, low, finish):
        def step(i, carry):
            def left(ref):
                return jnp.concatenate(
                    [ref[pl.ds(pl.multiple_of((i * PER + d + halo) * rows, 16), PER * rows), :]
                     for d in range(-reach, reach + 1)], axis=1)
            left_h, left_l = left(sh), left(sl)
            value = mul(left_h, high[...]) + mul(left_h, low[...]) + mul(left_l, high[...])
            finish(pl.ds(pl.multiple_of(i * PER * rows, 8), PER * rows), value)
            return carry
        lax.fori_loop(0, PARTS // PER, step, 0)

    def put(ref):
        def finish(at, value):
            ref[at, :] = value
        return finish

    v_first = vrows[...].astype(BF)
    v_rest = vrows[...] - v_first.astype(F32)
    v_second = v_rest.astype(BF)
    v_third = (v_rest - v_second.astype(F32)).astype(BF)
    v_stack = jnp.concatenate([v_first, v_second, v_third], axis=0)
    for c in range(PARTS):
        lanes = slice(c * CHUNK, (c + 1) * CHUNK)
        vs[c * rows:(c + 1) * rows, :] = mul(ex3, v_stack[:, lanes])
        fill(c, xs[:, lanes])
    planes(n_kin, wkh, wkl, put(kyz))
    for c in range(PARTS):
        high, low = split(xs[:, c * CHUNK:(c + 1) * CHUNK])
        one = mul(xl1[...], high)
        two = mul(xl2[...], low)
        fill(c, one[:rows] + one[rows:2 * rows] + two[:rows])
        kx[c * rows:(c + 1) * rows, :] = one[2 * rows:3 * rows] + one[3 * rows:] + two[rows:]

    def with_potential(at, value):
        tt[at, :] = value * vs[at, :]
    planes(n_mag, wfh, wfl, with_potential)
    for c in range(PARTS):
        fill(c, tt[c * rows:(c + 1) * rows, :])
    planes(n_mag, wbh, wbl, put(tt))
    for c in range(PARTS):
        at = slice(c * rows, (c + 1) * rows)
        high, low = split(tt[at, :])
        one = mul(xb1[...], high)
        xs[:, c * CHUNK:(c + 1) * CHUNK] = (
            one[:rows] + one[rows:] + mul(xb1[:rows, :], low) + kx[at, :] + kyz[at, :])
    for x in range(G):
        at, stop = x * plane, (x + 1) * plane
        while at < stop:
            d = at // cols
            until = min(stop, (d + 1) * cols)
            hbuf[d, :, at - d * cols:until - d * cols] = xs[
                x * own:(x + 1) * own, at - x * plane:until - x * plane]
            at = until

    h_start()
    own_h = pltpu.make_async_copy(hbuf.at[member], hc.at[member], lsem.at[1])
    own_h.start()

    def take(group):
        for r in range(group * per_tile, (group + 1) * per_tile):
            if r > 0:
                psi_copy(n - r).wait_recv()
        for r in range(group * per_tile, (group + 1) * per_tile):
            pf[(r % per_tile) * own:(r % per_tile + 1) * own, :] = pc[r]
        at = slice(group * per_tile * own, (group + 1) * per_tile * own)
        pm_h[at, :], pm_l[at, :] = split(pf[...])

    groups = n // per_tile
    for group in range(groups - 1, 0, -1):
        take(group)
    own_h.wait()
    h_arrive()
    for t in range(n_half):
        hm[t * own:(t + 1) * own, :] = hc[t]
    half_rows = n_half * own
    hs[:half_rows, :], hs[half_rows:, :] = split(hm[...])
    take(0)
    nt = (((1,), (1,)), ((), ()))

    def mul_t(left, right):
        return lax.dot_general(left, right, nt, preferred_element_type=F32)
    both = mul_t(hs[...], pm_h[...])
    part = (both[:half_rows] + both[half_rows:] + mul_t(hs[:half_rows, :], pm_l[...])) * (1.0 / NC)
    part = pltpu.roll(part, me * own, 1)
    for t in range(n_half):
        mp[t] = part[t * own:(t + 1) * own, :]

    r_start()
    red[member] = mp[member]
    r_arrive()
    mrow[...] = jnp.sum(red[...], axis=0)
    b_start()
    mall[member] = mrow[...]
    b_arrive()
    margin_t = jnp.concatenate([mall[t] for t in range(n_half)], axis=0)
    margin_t = pltpu.roll(margin_t, lax.rem(total - me * own, total), 1)
    m_both = jnp.concatenate(split(margin_t), axis=0)
    own_g = []
    for c in range(pieces):
        lanes = slice(c * wide, (c + 1) * wide)
        turned = mul(m_both, pm_h[:, lanes])
        value = hm[:, lanes] - (
            turned[:half_rows] + turned[half_rows:] + mul(m_both[:half_rows], pm_l[:, lanes]))
        for t in range(n_half):
            gbuf[c, t] = value[t * own:(t + 1) * own, :]
        g_pieces[c][0]()
        copy = pltpu.make_async_copy(
            gbuf.at[c, member], out_ref.at[:, pl.ds(pl.multiple_of(member * cols + c * wide, 128), wide)],
            lsem.at[2 + c])
        copy.start()
        own_g.append(copy)
    p_sent()
    h_sent()
    r_sent()
    b_sent()
    for c in range(pieces):
        own_g[c].wait()
        g_pieces[c][1]()
        g_pieces[c][2]()


def shards(n_orb, n_pan, orbitals, potential, magic_taps, kinetic_taps):
    own, width = orbitals.shape
    n, n_half = n_orb * n_pan, n_orb * (n_pan // 2)
    cols = width // n_half
    rows, total = G * own, n * own
    pieces = 3 if cols % (3 * 128) == 0 else 1
    per_tile = math.gcd(n, -(-16 // own))
    n_mag, n_kin = block_range(magic_taps.shape[0]), block_range(kinetic_taps.shape[0])
    halo = max(n_mag, n_kin)
    lane = np.arange(CHUNK)
    ez3, ezt = one_hot(lane, 3), one_hot(lane).T
    ey3 = jnp.stack([one_hot(lane // G + UNIT * d, 3) for d in range(-halo, halo + 1)])
    eyt = one_hot(lane // G).T
    row = np.arange(rows)
    ex3, ext = one_hot(row // own, 3), one_hot(row // own).T
    same = jnp.asarray((row[:, None] % own == row[None, :] % own).astype(np.float32))
    vmem = pl.BlockSpec(memory_space=pltpu.VMEM)
    span_m, span_k = (2 * n_mag + 1) * CHUNK, (2 * n_kin + 1) * CHUNK
    chunked = pltpu.VMEM((PARTS * rows, CHUNK), F32)
    halved = pltpu.VMEM(((PARTS + 2 * halo) * rows, CHUNK), BF)
    smem = pl.BlockSpec(memory_space=pltpu.SMEM)
    blocks = pltpu.VMEM((n_half, own, cols), F32)
    dma = pltpu.SemaphoreType.DMA
    return pl.pallas_call(
        functools.partial(kernel, n_orb, n_pan, own, cols, n_mag, n_kin, pieces, per_tile),
        out_shape=jax.ShapeDtypeStruct((own, width), F32),
        in_specs=[pl.BlockSpec(memory_space=pl.ANY), vmem] + [smem] * 2 + [vmem] * 7,
        out_specs=pl.BlockSpec(memory_space=OUT_SPACE),
        scratch_shapes=[
            pltpu.VMEM((span_m, CHUNK), BF), pltpu.VMEM((span_m, CHUNK), BF),
            pltpu.VMEM((span_m, CHUNK), BF), pltpu.VMEM((span_m, CHUNK), BF),
            pltpu.VMEM((span_k, CHUNK), BF), pltpu.VMEM((span_k, CHUNK), BF),
            pltpu.VMEM((4 * rows, rows), BF), pltpu.VMEM((2 * rows, rows), BF), pltpu.VMEM((2 * rows, rows), BF),
            halved, halved,
            pltpu.VMEM((rows, G * G), F32), chunked, chunked, chunked, chunked,
            pltpu.VMEM((G, G * G), F32),
            pltpu.VMEM((own, width), F32), blocks, pltpu.VMEM((n, own, cols), F32), blocks,
            pltpu.VMEM((total, cols), BF), pltpu.VMEM((total, cols), BF), pltpu.VMEM((per_tile * own, cols), F32),
            pltpu.VMEM((n_half * own, cols), F32), pltpu.VMEM((2 * n_half * own, cols), BF),
            pltpu.VMEM((pieces, n_half, own, cols // pieces), F32),
            pltpu.VMEM((n_half, own, total), F32), pltpu.VMEM((n_half, own, total), F32),
            pltpu.VMEM((own, total), F32), pltpu.VMEM((n_half, own, total), F32),
            dma((n,)), dma((n,)), dma((n_half,)), dma((n_half,)), dma((n_half,)), dma((n_half,)), dma((n_half,)),
            dma((n_half,)), dma((pieces, n_half)), dma((pieces, n_half)), dma((2 + pieces,)),
        ],
        compiler_params=pltpu.CompilerParams(
            collective_id=0, has_side_effects=True, vmem_limit_bytes=60 * 1024 * 1024),
    )(orbitals, potential.reshape(1, width), magic_taps, kinetic_taps, ez3, ezt, ey3, eyt, ex3, ext, same)


OUT_SPACE = pl.ANY


def solution(mesh):
    placed = (P(("orb", "pan"), None), P(), P(), P())
    n_pan = mesh.shape["pan"]
    n_orb = mesh.shape["orb"]
    aligned = n_pan % 2 == 0 and NC % (n_orb * (n_pan // 2) * 128) == 0
    body = functools.partial(shards, n_orb, n_pan) if aligned else plain_shards
    return jax.shard_map(
        body, mesh=mesh, in_specs=placed, out_specs=P(("orb", "pan"), None), check_vma=False
    )
```
